128 devices in a mesh: band: 16 (over z, y), lon: 8 (over x, core).
Axes of the slice: x: 4, y: 4, z: 4, core: 2. Of those that a mesh axis runs over, the one named last changes fastest.
Arguments:
- background: float32 [2, 16, 1024, 256], P(None, None, ('lon', 'band')), may hold values from -6 to 6
- scale_x: float32 [16, 1024, 256], P(None, ('lon', 'band')), may hold values from 0.04 to 0.24
- scale_y: float32 [16, 1024, 256], P(None, ('lon', 'band')), may hold values from 0.04 to 0.24
- filter_bands: float32 [2, 5, 16], replicated, may hold values from -0.3 to 0.3
- band_rows: int32 [16], replicated, may hold values from 8 to 32, as said below
Outputs:
- increment: float32 [2, 16, 1024, 256], P(None, None, ('lon', 'band'))
- band_field: float32 [2, 16, 512, 1024], P(None, None, 'band', 'lon')
The draws below stay inside these ranges and needn't reach their ends.
Inputs may be any that keep to these rules, and one draw needn't show every extreme that they name: `band_rows`: bands follow one another from the first row and their rows sum to 256; one band has exactly 32 rows and one exactly 8 rows.
All inputs are finite; a program needn't handle non-finite values.
Results may differ from the reference program's by a relative error of at most 0.0003.
Values sent between devices are 32-bit elements; how exact they have to be, the bound alone decides.
A program may use at most 64 MiB of HBM per device.

```python
import math
import jax
import jax.numpy as jnp
from jax import lax

VARS = 2
LEVELS = 16
STEPS = 8
EDGE = 8
BAND_MEAN = 16
CAP = 32
NY = 256
NX = 1024
N_BAND = 16


def draw_band_rows(key, part):
    first_key, second_key = jax.random.split(jax.random.fold_in(key, 7))
    others = N_BAND - 2
    spread_rows = BAND_MEAN // 8
    rough = jax.random.randint(first_key, (others,), 0, spread_rows + 1)
    rest = others * BAND_MEAN - EDGE
    base = rest // others
    remain = rest % others
    index = jnp.arange(others)
    change = rough - jnp.roll(rough, -1)
    middle = base + (index < remain).astype(jnp.int32) + change
    values = jnp.concatenate([jnp.array([CAP, EDGE], jnp.int32), middle.astype(jnp.int32)])
    places = jax.random.permutation(second_key, N_BAND)
    lengths = jnp.zeros((N_BAND,), jnp.int32).at[places].set(values)
    return lengths.astype(jnp.int32)


def level_of(stream_key, shape, cuts, smallest, largest):
    level, own = 1.0, jax.random.fold_in(stream_key, 6)
    for position, parts in cuts:
        steps = jnp.exp(jax.random.uniform(jax.random.fold_in(own, position), (parts,), jnp.float32, smallest / len(cuts), largest / len(cuts)))
        level = level * jnp.repeat(steps, shape[position] // parts).reshape([-1 if axis == position else 1 for axis in range(len(shape))])
    return level


def noise(key, shape, scale, reach, shards=(), held_as=jnp.bfloat16):
    entries = scale * jax.random.normal(key, shape, jnp.float32)
    if shards:
        entries = entries * level_of(key, shape, shards, -0.22, 0.18)
    return jnp.clip(entries, -reach, reach).astype(held_as)


def setup_inputs(seed: int = 0) -> dict:
    seeds = jax.random.split(jax.random.key(seed), 6)
    return {
        "background": noise(seeds[0], (VARS, LEVELS, NX, NY), 1.0, 6.0, ((2, 128),), jnp.float32),
        "scale_x": jnp.clip(jnp.exp(math.log(0.24) - 1.7917595 * jax.random.uniform(seeds[1], (LEVELS, NX, NY), jnp.float32) ** level_of(seeds[1], (LEVELS, NX, NY), ((1, 128),), -0.2, 0.2)), 0.04, 0.24),
        "scale_y": jnp.clip(jnp.exp(math.log(0.24) - 1.7917595 * jax.random.uniform(seeds[2], (LEVELS, NX, NY), jnp.float32) ** level_of(seeds[2], (LEVELS, NX, NY), ((1, 128),), -0.2, 0.2)), 0.04, 0.24),
        "filter_bands": jnp.clip(jax.random.uniform(seeds[3], (VARS, 5, LEVELS), jnp.float32, -0.3, 0.3), -0.3, 0.3),
        "band_rows": draw_band_rows(jax.random.fold_in(seeds[5], 71), 0),
    }


def spread(field, along_x, along_y, x_axis, y_axis):
    flux_x = along_x * (jnp.roll(field, -1, x_axis) - field)
    flux_y = along_y * (jnp.roll(field, -1, y_axis) - field)
    return field + flux_x - jnp.roll(flux_x, 1, x_axis) + flux_y - jnp.roll(flux_y, 1, y_axis)


def vertical(field, filter_bands):
    levels = field.shape[1]
    padded = jnp.pad(field, ((0, 0), (2, 2), (0, 0), (0, 0)))
    total = field
    for offset in range(5):
        weight = filter_bands[:, offset, :][:, :, None, None]
        total = total + weight * padded[:, offset:offset + levels]
    return total


def reference(background, scale_x, scale_y, filter_bands, band_rows):
    rows = background.shape[3]
    along_y = scale_y * (jnp.arange(rows) < rows - 1).astype(jnp.float32)
    field = background
    for step in range(STEPS):
        field = spread(field, scale_x, along_y, 2, 3)
    increment = vertical(field, filter_bands)
    starts = (jnp.cumsum(band_rows) - band_rows).astype(jnp.int32)
    padded = jnp.pad(increment, ((0, 0), (0, 0), (0, 0), (0, CAP)))

    def one_band(pair):
        piece = lax.dynamic_slice_in_dim(padded, pair[0], CAP, 3)
        keep = (jnp.arange(CAP) < pair[1]).astype(jnp.float32)
        return piece * keep

    bands = lax.map(one_band, (starts, band_rows.astype(jnp.int32)))
    band_field = jnp.transpose(bands, (1, 2, 0, 4, 3)).reshape(VARS, LEVELS, N_BAND * CAP, background.shape[2])
    return increment, band_field
```

```python
import functools

import jax
import jax.numpy as jnp
from jax import lax
from jax.experimental import pallas as pl
from jax.experimental.pallas import tpu as pltpu
from jax.sharding import PartitionSpec as P

MESH = pl.DeviceIdType.MESH
STEPS = 8
CAP = 32
DEPTH = 4
ROUNDS = STEPS // DEPTH
WIDTH = 8
LANES = 128
SX, SY = 2, 3


def roll(x, shift):
    return pltpu.roll(x, shift, x.ndim - 1)


def diffuse(get_field, get_sx, get_sy, put, lane):
    last, first = lane == LANES - 1, lane == 0
    held = [None] * DEPTH
    flux = [None] * DEPTH

    def push(step, column, field):
        if step == DEPTH:
            put(column, field)
            return
        before, west = held[step], flux[step]
        held[step] = field
        if before is None:
            return
        p = column - 1
        sx = get_sx(p)
        east = [sx[i] * (field[i] - before[i]) for i in range(2)]
        flux[step] = east
        if west is None:
            return
        sy = get_sy(p)
        ra, rb = roll(before[0], LANES - 1), roll(before[1], LANES - 1)
        up = [jnp.where(last, rb, ra), rb]
        north = [sy[i] * (up[i] - before[i]) for i in range(2)]
        qa, qb = roll(north[0], 1), roll(north[1], 1)
        south = [jnp.where(first, qb, qa), jnp.where(first, qa, qb)]
        new = [before[i] + east[i] - west[i] + north[i] - south[i] for i in range(2)]
        push(step + 1, p, new)

    for column in range(-DEPTH, WIDTH + DEPTH):
        push(0, column, get_field(column))


def kernel(
    rows_ref, filt_ref, bg_ref, sx_ref, sy_ref,
    inc_ref, bf_ref,
    raw_bg, raw_sx, raw_sy, own, halo0, halo1, mid, done, nat, out_inc,
    send_buf, recv_buf, band_nat, out_bf, st,
    in_sem, hs_sem, hr_sem, as_sem, ar_sem, out_sem,
):
    n_band, n_lon = lax.axis_size("band"), lax.axis_size("lon")
    band, lon = lax.axis_index("band"), lax.axis_index("lon")
    at_end, at_start = band == n_band - 1, band == 0
    right = (
        jnp.where(at_end, 0, band + 1),
        jnp.where(at_end, lax.rem(lon + 1, n_lon), lon),
    )
    left = (
        jnp.where(at_start, n_band - 1, band - 1),
        jnp.where(at_start, lax.rem(lon + n_lon - 1, n_lon), lon),
    )

    def peer(k):
        z = lax.rem(band // 4 + k // 4, 4)
        y = lax.rem(lax.rem(band, 4) + lax.rem(k, 4), 4)
        return z * 4 + y

    barrier = pltpu.get_barrier_semaphore()
    for side in (left, right):
        pl.semaphore_signal(barrier, inc=1, device_id=side, device_id_type=MESH)

    def greet(k, carry):
        pl.semaphore_signal(
            barrier, inc=1, device_id=(peer(k), lon), device_id_type=MESH
        )
        return carry

    lax.fori_loop(1, n_band, greet, 0)

    copies = []
    for ref, raw in ((bg_ref, raw_bg), (sx_ref, raw_sx), (sy_ref, raw_sy)):
        for half in range(2):
            copies.append(
                pltpu.make_async_copy(
                    ref.at[:, pl.ds(half * LANES, LANES)],
                    raw.at[half],
                    in_sem.at[len(copies)],
                )
            )
            copies[-1].start()

    total = jnp.int32(0)
    for b in range(16):
        st[b] = total
        total = total + rows_ref[b]

    lane = lax.broadcasted_iota(jnp.int32, (8, LANES), 1)
    lane2 = lax.broadcasted_iota(jnp.int32, (2, 8, LANES), 2)
    for copy in copies:
        copy.wait()
    for h in range(2):
        for c in range(WIDTH):
            for half in range(2):
                for v in range(2):
                    own[h, c, v, half] = raw_bg[half, pl.ds(v * 128 + h * 64 + c, 8, stride=8), :]
                own[h, c, SX, half] = raw_sx[half, pl.ds(h * 64 + c, 8, stride=8), :]
                face = raw_sy[half, pl.ds(h * 64 + c, 8, stride=8), :]
                if half == 1:
                    face = jnp.where(lane == LANES - 1, 0.0, face)
                own[h, c, SY, half] = face

    pl.semaphore_wait(barrier, 2 + 15)

    def halo_copies(r, h):
        src, dst = ((own, halo0), (mid, halo1))[r]
        return [
            pltpu.make_async_remote_copy(
                src_ref=src.at[h, pl.ds(0, DEPTH)],
                dst_ref=dst.at[h, 1],
                send_sem=hs_sem.at[r, h, 0],
                recv_sem=hr_sem.at[r, h, 1],
                device_id=left,
                device_id_type=MESH,
            ),
            pltpu.make_async_remote_copy(
                src_ref=src.at[h, pl.ds(WIDTH - DEPTH, DEPTH)],
                dst_ref=dst.at[h, 0],
                send_sem=hs_sem.at[r, h, 1],
                recv_sem=hr_sem.at[r, h, 0],
                device_id=right,
                device_id_type=MESH,
            ),
        ]

    for h in range(2):
        for copy in halo_copies(0, h):
            copy.start()

    def one_round(r, h):
        inner, halo = ((own, halo0), (mid, halo1))[r]

        def pick(mine, side, column, unit):
            if column < 0:
                at = (h, 0, column + DEPTH)
                ref = side
            elif column < WIDTH:
                at = (h, column)
                ref = mine
            else:
                at = (h, 1, column - WIDTH)
                ref = side
            return [ref[at + (unit, half)] for half in range(2)]

        def put(column, new):
            if r + 1 < ROUNDS:
                for half in range(2):
                    mid[h, column, :, half] = new[half]
                return
            for half in range(2):
                done[h, column, :, half] = new[half]
                for v in range(2):
                    nat[half, pl.ds(v * 128 + h * 64 + column, 8, stride=8), :] = new[half][v]

        diffuse(
            lambda column: pick(inner, halo, column, slice(0, 2)),
            lambda column: pick(own, halo0, column, SX),
            lambda column: pick(own, halo0, column, SY),
            put,
            lane,
        )

    for h in range(2):
        for copy in halo_copies(0, h):
            copy.wait_recv()
        one_round(0, h)
        for copy in halo_copies(1, h):
            copy.start()
    for h in range(2):
        for copy in halo_copies(1, h):
            copy.wait_recv()
        one_round(1, h)

    def window(b, keep):
        start = st[b]
        for c in range(WIDTH):
            parts = []
            for q in range(4):
                v, h = q // 2, q % 2
                x = jnp.where(lane >= start, done[h, c, v, 0], done[h, c, v, 1])
                parts.append(roll(x, (32 * q + 256 - start) & 127))
            keep(
                c,
                jnp.where(
                    lane < 64,
                    jnp.where(lane < 32, parts[0], parts[1]),
                    jnp.where(lane < 96, parts[2], parts[3]),
                ),
            )

    def band_copy(k):
        return pltpu.make_async_remote_copy(
            src_ref=send_buf.at[k],
            dst_ref=recv_buf.at[pl.ds(pl.multiple_of(band * 64, 64), 64)],
            send_sem=as_sem.at[k],
            recv_sem=ar_sem.at[k],
            device_id=(peer(k), lon),
            device_id_type=MESH,
        )

    def send(k, carry):
        def keep(c, value):
            send_buf[k, pl.ds(c * 8, 8), :] = value

        window(peer(k), keep)
        band_copy(k).start()
        return carry

    lax.fori_loop(1, n_band, send, 0)

    def keep_own(c, value):
        recv_buf[pl.ds(pl.multiple_of(band * 64 + c * 8, 8), 8), :] = value

    window(band, keep_own)

    for v in range(2):
        for level in range(16):
            for half in range(2):
                rows = v * 128 + level * 8
                value = nat[half, rows:rows + 8, :]
                for o in range(5):
                    if 0 <= level + o - 2 < 16:
                        near = rows + (o - 2) * 8
                        value = value + filt_ref[o, v, level] * nat[half, near:near + 8, :]
                out_inc[rows:rows + 8, half * LANES:(half + 1) * LANES] = value
    put_inc = pltpu.make_async_copy(out_inc, inc_ref, out_sem.at[0])
    put_inc.start()

    def arrive(k, carry):
        band_copy(k).wait_recv()
        return carry

    lax.fori_loop(1, n_band, arrive, 0)

    for s in range(8):
        flat = recv_buf[pl.ds(s, LANES, stride=8), :].T
        for q in range(4):
            v, h = q // 2, q % 2
            band_nat[v, h * 8 + s] = flat[q * CAP:(q + 1) * CAP, :]
    inside = lax.broadcasted_iota(jnp.int32, (CAP, LANES), 0) < rows_ref[band]
    outs = []
    for v in range(2):
        for level in range(16):
            value = band_nat[v, level]
            for o in range(5):
                if 0 <= level + o - 2 < 16:
                    value = value + filt_ref[o, v, level] * band_nat[v, level + o - 2]
            rows = (v * 16 + level) * CAP
            out_bf[rows:rows + CAP, :] = jnp.where(inside, value, 0.0)
        copy = pltpu.make_async_copy(
            out_bf.at[pl.ds(v * 512, 512)], bf_ref.at[pl.ds(v * 512, 512)], out_sem.at[1 + v]
        )
        copy.start()
        outs.append(copy)

    for r in range(ROUNDS):
        for h in range(2):
            for copy in halo_copies(r, h):
                copy.wait_send()

    def sent(k, carry):
        band_copy(k).wait_send()
        return carry

    lax.fori_loop(1, n_band, sent, 0)
    put_inc.wait()
    for copy in outs:
        copy.wait()


def shards(background, scale_x, scale_y, filter_bands, band_rows):
    f32 = jnp.float32
    any_space = pl.BlockSpec(memory_space=pl.ANY)
    smem = pl.BlockSpec(memory_space=pltpu.SMEM)
    vmem = pltpu.VMEM
    dma = pltpu.SemaphoreType.DMA
    inc, bf = pl.pallas_call(
        kernel,
        out_shape=(
            jax.ShapeDtypeStruct((256, 256), f32),
            jax.ShapeDtypeStruct((1024, LANES), f32),
        ),
        in_specs=[smem, smem, any_space, any_space, any_space],
        out_specs=(any_space, any_space),
        scratch_shapes=[
            vmem((2, 256, LANES), f32),
            vmem((2, 128, LANES), f32),
            vmem((2, 128, LANES), f32),
            vmem((2, WIDTH, 4, 2, 8, LANES), f32),
            vmem((2, 2, DEPTH, 4, 2, 8, LANES), f32),
            vmem((2, 2, DEPTH, 2, 2, 8, LANES), f32),
            vmem((2, WIDTH, 2, 2, 8, LANES), f32),
            vmem((2, WIDTH, 2, 2, 8, LANES), f32),
            vmem((2, 256, LANES), f32),
            vmem((256, 256), f32),
            vmem((16, 64, LANES), f32),
            vmem((1024, LANES), f32),
            vmem((2, 16, CAP, LANES), f32),
            vmem((1024, LANES), f32),
            pltpu.SMEM((16,), jnp.int32),
            dma((6,)),
            dma((ROUNDS, 2, 2)),
            dma((ROUNDS, 2, 2)),
            dma((16,)),
            dma((16,)),
            dma((3,)),
        ],
        compiler_params=pltpu.CompilerParams(collective_id=0, has_side_effects=True),
    )(
        band_rows,
        jnp.transpose(filter_bands, (1, 0, 2)),
        background.reshape(256, 256),
        scale_x.reshape(128, 256),
        scale_y.reshape(128, 256),
    )
    return inc.reshape(background.shape), bf.reshape(2, 16, CAP, LANES)


def solution(mesh):
    strips = P(None, None, ("lon", "band"), None)
    faces = P(None, ("lon", "band"), None)
    return jax.shard_map(
        shards,
        mesh=mesh,
        in_specs=(strips, faces, faces, P(), P()),
        out_specs=(strips, P(None, None, "band", "lon")),
        check_vma=False,
    )
```

```python
import functools

import jax
import jax.numpy as jnp
from jax import lax
from jax.experimental import pallas as pl
from jax.experimental.pallas import tpu as pltpu
from jax.sharding import PartitionSpec as P

MESH = pl.DeviceIdType.MESH
STEPS = 8
CAP = 32
DEPTH = 8
ROUNDS = STEPS // DEPTH
WIDTH = 8
LANES = 128
SX, SY = 2, 3


def roll(x, shift):
    return pltpu.roll(x, shift, x.ndim - 1)


def diffuse(get_field, get_sx, get_sy, put, lane):
    last, first = lane == LANES - 1, lane == 0
    held = [None] * DEPTH
    flux = [None] * DEPTH

    def push(step, column, field):
        if step == DEPTH:
            put(column, field)
            return
        before, west = held[step], flux[step]
        held[step] = field
        if before is None:
            return
        p = column - 1
        sx = get_sx(p)
        east = [sx[i] * (field[i] - before[i]) for i in range(2)]
        flux[step] = east
        if west is None:
            return
        sy = get_sy(p)
        ra, rb = roll(before[0], LANES - 1), roll(before[1], LANES - 1)
        up = [jnp.where(last, rb, ra), rb]
        north = [sy[i] * (up[i] - before[i]) for i in range(2)]
        qa, qb = roll(north[0], 1), roll(north[1], 1)
        south = [jnp.where(first, qb, qa), jnp.where(first, qa, qb)]
        new = [before[i] + east[i] - west[i] + north[i] - south[i] for i in range(2)]
        push(step + 1, p, new)

    for column in range(-DEPTH, WIDTH + DEPTH):
        push(0, column, get_field(column))


def torus(band):
    z, y = band // 4, lax.rem(band, 4)
    return [
        lax.rem(z + 1, 4) * 4 + y,
        lax.rem(z + 3, 4) * 4 + y,
        z * 4 + lax.rem(y + 1, 4),
        z * 4 + lax.rem(y + 3, 4),
    ]


def strips_kernel(
    rows_ref, bg_ref, sx_ref, sy_ref,
    win_ref, nat_ref,
    raw_bg, raw_sx, raw_sy, own, halo0, halo1, mid, done, send_buf, rows, st,
    near_sem, in_sem, hs_sem, hr_sem, as_sem, ar_sem,
):
    n_band, n_lon = lax.axis_size("band"), lax.axis_size("lon")
    band, lon = lax.axis_index("band"), lax.axis_index("lon")
    at_end, at_start = band == n_band - 1, band == 0
    right = (
        jnp.where(at_end, 0, band + 1),
        jnp.where(at_end, lax.rem(lon + 1, n_lon), lon),
    )
    left = (
        jnp.where(at_start, n_band - 1, band - 1),
        jnp.where(at_start, lax.rem(lon + n_lon - 1, n_lon), lon),
    )
    near = [(b, lon) for b in torus(band)]

    barrier = pltpu.get_barrier_semaphore()
    for side in [left, right] + near:
        pl.semaphore_signal(barrier, inc=1, device_id=side, device_id_type=MESH)

    copies = []
    for ref, raw in ((bg_ref, raw_bg), (sx_ref, raw_sx), (sy_ref, raw_sy)):
        for half in range(2):
            copies.append(
                pltpu.make_async_copy(
                    ref.at[:, pl.ds(half * LANES, LANES)],
                    raw.at[half],
                    in_sem.at[len(copies)],
                )
            )
    copies.append(pltpu.make_async_copy(rows_ref, rows, in_sem.at[len(copies)]))
    for copy in copies:
        copy.start()

    lane = lax.broadcasted_iota(jnp.int32, (8, LANES), 1)
    for copy in copies:
        copy.wait()
    for h in range(2):
        for c in range(WIDTH):
            for half in range(2):
                for v in range(2):
                    own[h, c, v, half] = raw_bg[half, pl.ds(v * 128 + h * 64 + c, 8, stride=8), :]
                own[h, c, SX, half] = raw_sx[half, pl.ds(h * 64 + c, 8, stride=8), :]
                face = raw_sy[half, pl.ds(h * 64 + c, 8, stride=8), :]
                if half == 1:
                    face = jnp.where(lane == LANES - 1, 0.0, face)
                own[h, c, SY, half] = face

    pl.semaphore_wait(barrier, 6)

    def halo_copies(r, h):
        src, dst = ((own, halo0), (mid, halo1))[r]
        return [
            pltpu.make_async_remote_copy(
                src_ref=src.at[h, pl.ds(0, DEPTH)],
                dst_ref=dst.at[h, 1],
                send_sem=hs_sem.at[r, h, 0],
                recv_sem=hr_sem.at[r, h, 1],
                device_id=left,
                device_id_type=MESH,
            ),
            pltpu.make_async_remote_copy(
                src_ref=src.at[h, pl.ds(WIDTH - DEPTH, DEPTH)],
                dst_ref=dst.at[h, 0],
                send_sem=hs_sem.at[r, h, 1],
                recv_sem=hr_sem.at[r, h, 0],
                device_id=right,
                device_id_type=MESH,
            ),
        ]

    for h in range(2):
        for copy in halo_copies(0, h):
            copy.start()

    for hop in range(3):
        for peer in near:
            pl.semaphore_signal(
                near_sem.at[hop], inc=1, device_id=peer, device_id_type=MESH
            )
        pl.semaphore_wait(near_sem.at[hop], 4)

    total = jnp.int32(0)
    for b in range(16):
        st[b] = total
        total = total + rows[b]

    def one_round(r, h):
        inner, halo = ((own, halo0), (mid, halo1))[r]

        def pick(mine, side, column, unit):
            if column < 0:
                at = (h, 0, column + DEPTH)
                ref = side
            elif column < WIDTH:
                at = (h, column)
                ref = mine
            else:
                at = (h, 1, column - WIDTH)
                ref = side
            return [ref[at + (unit, half)] for half in range(2)]

        def put(column, new):
            if r + 1 < ROUNDS:
                for half in range(2):
                    mid[h, column, :, half] = new[half]
                return
            for half in range(2):
                done[h, column, :, half] = new[half]
                for v in range(2):
                    nat_ref[half, pl.ds(v * 128 + h * 64 + column, 8, stride=8), :] = new[half][v]

        diffuse(
            lambda column: pick(inner, halo, column, slice(0, 2)),
            lambda column: pick(own, halo0, column, SX),
            lambda column: pick(own, halo0, column, SY),
            put,
            lane,
        )

    for r in range(ROUNDS):
        for h in range(2):
            for copy in halo_copies(r, h):
                copy.wait_recv()
            one_round(r, h)
            if r + 1 < ROUNDS:
                for copy in halo_copies(r + 1, h):
                    copy.start()

    def slot(b):
        return win_ref.at[pl.ds(pl.multiple_of(b * 64, 64), 64)]

    def target(i):
        return i // 4 * 4 + lax.rem(lax.rem(band, 4) + lax.rem(i, 4), 4)

    def band_copy(i):
        return pltpu.make_async_remote_copy(
            src_ref=send_buf.at[i],
            dst_ref=slot(band),
            send_sem=as_sem.at[i],
            recv_sem=ar_sem.at[band],
            device_id=(target(i), lon),
            device_id_type=MESH,
        )

    def send(i, carry):
        b = target(i)
        start = st[b]
        for c in range(WIDTH):
            parts = []
            for q in range(4):
                v, h = q // 2, q % 2
                x = jnp.where(lane >= start, done[h, c, v, 0], done[h, c, v, 1])
                parts.append(roll(x, (32 * q + 256 - start) & 127))
            send_buf[i, pl.ds(c * 8, 8), :] = jnp.where(
                lane < 64,
                jnp.where(lane < 32, parts[0], parts[1]),
                jnp.where(lane < 96, parts[2], parts[3]),
            )

        @pl.when(b != band)
        def _():
            band_copy(i).start()

        @pl.when(b == band)
        def _():
            pltpu.make_async_copy(send_buf.at[i], slot(band), ar_sem.at[band]).start()

        return carry

    lax.fori_loop(0, n_band, send, 0)

    for r in range(ROUNDS):
        for h in range(2):
            for copy in halo_copies(r, h):
                copy.wait_send()

    def arrive(b, carry):
        pltpu.make_async_copy(send_buf.at[0], slot(b), ar_sem.at[b]).wait()
        return carry

    lax.fori_loop(0, n_band, arrive, 0)

    def sent(i, carry):
        @pl.when(target(i) != band)
        def _():
            band_copy(i).wait_send()

        return carry

    lax.fori_loop(0, n_band, sent, 0)


def filter_kernel(
    rows_ref, filt_ref, win_ref, nat_ref, inc_ref, bf_ref,
    rows, filt, band_nat, out_inc, out_bf, in_sem, out_sem,
):
    scalars = [
        pltpu.make_async_copy(rows_ref, rows, in_sem.at[0]),
        pltpu.make_async_copy(filt_ref, filt, in_sem.at[1]),
    ]
    for copy in scalars:
        copy.start()
    for s in range(8):
        flat = win_ref[pl.ds(s, LANES, stride=8), :].T
        for q in range(4):
            v, h = q // 2, q % 2
            band_nat[v, h * 8 + s] = flat[q * CAP:(q + 1) * CAP, :]
    for copy in scalars:
        copy.wait()

    inside = lax.broadcasted_iota(jnp.int32, (CAP, LANES), 0) < rows[lax.axis_index("band")]
    outs = []
    for v in range(2):
        for level in range(16):
            value = band_nat[v, level]
            for o in range(5):
                if 0 <= level + o - 2 < 16:
                    value = value + filt[o, v, level] * band_nat[v, level + o - 2]
            at = (v * 16 + level) * CAP
            out_bf[at:at + CAP, :] = jnp.where(inside, value, 0.0)
        outs.append(
            pltpu.make_async_copy(
                out_bf.at[pl.ds(v * 512, 512)], bf_ref.at[pl.ds(v * 512, 512)], out_sem.at[v]
            )
        )
        outs[-1].start()

    for v in range(2):
        for level in range(16):
            for half in range(2):
                at = v * 128 + level * 8
                value = nat_ref[half, at:at + 8, :]
                for o in range(5):
                    if 0 <= level + o - 2 < 16:
                        beside = at + (o - 2) * 8
                        value = value + filt[o, v, level] * nat_ref[half, beside:beside + 8, :]
                out_inc[at:at + 8, half * LANES:(half + 1) * LANES] = value
    outs.append(pltpu.make_async_copy(out_inc, inc_ref, out_sem.at[2]))
    outs[-1].start()
    for copy in outs:
        copy.wait()


def shards(background, scale_x, scale_y, filter_bands, band_rows):
    f32 = jnp.float32
    any_space = pl.BlockSpec(memory_space=pl.ANY)
    hbm = pl.BlockSpec(memory_space=pltpu.HBM)
    resident = pl.BlockSpec(memory_space=pltpu.VMEM)
    vmem = pltpu.VMEM
    dma = pltpu.SemaphoreType.DMA
    win, nat = pl.pallas_call(
        strips_kernel,
        out_shape=(
            jax.ShapeDtypeStruct((1024, LANES), f32),
            jax.ShapeDtypeStruct((2, 256, LANES), f32),
        ),
        in_specs=[any_space, hbm, hbm, hbm],
        out_specs=(resident, resident),
        scratch_shapes=[
            vmem((2, 256, LANES), f32),
            vmem((2, 128, LANES), f32),
            vmem((2, 128, LANES), f32),
            vmem((2, WIDTH, 4, 2, 8, LANES), f32),
            vmem((2, 2, DEPTH, 4, 2, 8, LANES), f32),
            vmem((2, 2, DEPTH, 2, 2, 8, LANES), f32),
            vmem((2, WIDTH, 2, 2, 8, LANES), f32),
            vmem((2, WIDTH, 2, 2, 8, LANES), f32),
            vmem((16, 64, LANES), f32),
            pltpu.SMEM((16,), jnp.int32),
            pltpu.SMEM((16,), jnp.int32),
            pltpu.SemaphoreType.REGULAR((3,)),
            dma((7,)),
            dma((ROUNDS, 2, 2)),
            dma((ROUNDS, 2, 2)),
            dma((16,)),
            dma((16,)),
        ],
        compiler_params=pltpu.CompilerParams(
            collective_id=0, has_side_effects=True, vmem_limit_bytes=16 << 20
        ),
    )(
        pltpu.with_memory_space_constraint(band_rows, pltpu.HBM),
        pltpu.with_memory_space_constraint(background.reshape(256, 256), pltpu.HBM),
        pltpu.with_memory_space_constraint(scale_x.reshape(128, 256), pltpu.HBM),
        pltpu.with_memory_space_constraint(scale_y.reshape(128, 256), pltpu.HBM),
    )
    inc, bf = pl.pallas_call(
        filter_kernel,
        out_shape=(
            jax.ShapeDtypeStruct((256, 256), f32),
            jax.ShapeDtypeStruct((1024, LANES), f32),
        ),
        in_specs=[any_space, any_space, resident, resident],
        out_specs=(hbm, hbm),
        scratch_shapes=[
            pltpu.SMEM((16,), jnp.int32),
            pltpu.SMEM((5, 2, 16), f32),
            vmem((2, 16, CAP, LANES), f32),
            vmem((256, 256), f32),
            vmem((1024, LANES), f32),
            dma((2,)),
            dma((3,)),
        ],
        compiler_params=pltpu.CompilerParams(vmem_limit_bytes=16 << 20),
    )(band_rows, jnp.transpose(filter_bands, (1, 0, 2)), win, nat)
    return inc.reshape(background.shape), bf.reshape(2, 16, CAP, LANES)


def solution(mesh):
    strips = P(None, None, ("lon", "band"), None)
    faces = P(None, ("lon", "band"), None)
    return jax.shard_map(
        shards,
        mesh=mesh,
        in_specs=(strips, faces, faces, P(), P()),
        out_specs=(strips, P(None, None, "band", "lon")),
        check_vma=False,
    )
```

```python
import jax
import jax.numpy as jnp
from jax import lax
from jax.experimental import pallas as pl
from jax.experimental.pallas import tpu as pltpu
from jax.sharding import PartitionSpec as P

MESH = pl.DeviceIdType.MESH
STEPS = 8
CAP = 32
WIDTH = 8
LANES = 128
LEFT, OWN, RIGHT = 0, 1, 2
SX, SY, VAR = 0, 1, 2


def roll(x, shift):
    return pltpu.roll(x, shift, x.ndim - 1)


def diffuse(get_field, get_sx, get_sy, put, lane):
    last, first = lane == LANES - 1, lane == 0
    held = [None] * STEPS
    flux = [None] * STEPS

    def push(step, column, field):
        if step == STEPS:
            put(column, field)
            return
        before, west = held[step], flux[step]
        held[step] = field
        if before is None:
            return
        p = column - 1
        sx = get_sx(p)
        east = [sx[i] * (field[i] - before[i]) for i in range(2)]
        flux[step] = east
        if west is None:
            return
        sy = get_sy(p)
        ra, rb = roll(before[0], LANES - 1), roll(before[1], LANES - 1)
        up = [jnp.where(last, rb, ra), rb]
        north = [sy[i] * (up[i] - before[i]) for i in range(2)]
        qa, qb = roll(north[0], 1), roll(north[1], 1)
        south = [jnp.where(first, qb, qa), jnp.where(first, qa, qb)]
        new = [before[i] + east[i] - west[i] + north[i] - south[i] for i in range(2)]
        push(step + 1, p, new)

    for column in range(-STEPS, WIDTH + STEPS):
        push(0, column, get_field(column))


def torus(band):
    z, y = band // 4, lax.rem(band, 4)
    return [
        lax.rem(z + 1, 4) * 4 + y,
        lax.rem(z + 3, 4) * 4 + y,
        z * 4 + lax.rem(y + 1, 4),
        z * 4 + lax.rem(y + 3, 4),
    ]


def strips_kernel(
    rows_ref, filt_ref, bg_ref, sx_ref, sy_ref,
    win_ref, inc_ref,
    raw, cols, done, nat, send_buf, rows, filt, st,
    near_sem, in_sem, hs_sem, hr_sem, as_sem, ar_sem,
):
    n_band, n_lon = lax.axis_size("band"), lax.axis_size("lon")
    band, lon = lax.axis_index("band"), lax.axis_index("lon")
    at_end, at_start = band == n_band - 1, band == 0
    right = (
        jnp.where(at_end, 0, band + 1),
        jnp.where(at_end, lax.rem(lon + 1, n_lon), lon),
    )
    left = (
        jnp.where(at_start, n_band - 1, band - 1),
        jnp.where(at_start, lax.rem(lon + n_lon - 1, n_lon), lon),
    )
    near = [(b, lon) for b in torus(band)]

    barrier = pltpu.get_barrier_semaphore()
    for side in [left, right] + near:
        pl.semaphore_signal(barrier, inc=1, device_id=side, device_id_type=MESH)

    copies = [
        pltpu.make_async_copy(sx_ref, raw.at[SX], in_sem.at[0]),
        pltpu.make_async_copy(sy_ref, raw.at[SY], in_sem.at[1]),
        pltpu.make_async_copy(bg_ref, raw.at[pl.ds(VAR, 2)], in_sem.at[2]),
    ]
    scalars = [
        pltpu.make_async_copy(rows_ref, rows, in_sem.at[3]),
        pltpu.make_async_copy(filt_ref, filt, in_sem.at[4]),
    ]
    for copy in copies + scalars:
        copy.start()

    def halo_copy(h, i, unit):
        device, strip = ((left, RIGHT), (right, LEFT))[i]
        first, count = 0, WIDTH
        if i == 0 and unit in (SX, SY):
            count = WIDTH - 1
        elif i == 1 and unit == SY:
            first, count = 1, WIDTH - 1
        return pltpu.make_async_remote_copy(
            src_ref=cols.at[OWN, h, unit, pl.ds(first, count)],
            dst_ref=cols.at[strip, h, unit, pl.ds(first, count)],
            send_sem=hs_sem.at[h, i, unit],
            recv_sem=hr_sem.at[h, i, unit],
            device_id=device,
            device_id_type=MESH,
        )

    lane = lax.broadcasted_iota(jnp.int32, (8, LANES), 1)
    for h in range(2):
        for unit in range(4):
            if h == 0 and unit < 3:
                copies[unit].wait()
            for c in range(WIDTH):
                for half in range(2):
                    tile = raw[unit, h, pl.ds(half * 8 + c, 8, stride=16), :]
                    if unit == SY and half == 1:
                        tile = jnp.where(lane == LANES - 1, 0.0, tile)
                    cols[OWN, h, unit, c, half] = tile
        if h == 0:
            pl.semaphore_wait(barrier, 6)
        for unit in range(4):
            for i in range(2):
                halo_copy(h, i, unit).start()

    for hop in range(3):
        for peer in near:
            pl.semaphore_signal(
                near_sem.at[hop], inc=1, device_id=peer, device_id_type=MESH
            )
        pl.semaphore_wait(near_sem.at[hop], 4)

    for copy in scalars:
        copy.wait()
    total = jnp.int32(0)
    for b in range(16):
        st[b] = total
        total = total + rows[b]

    def run_block(h, v):
        def load(unit, column):
            strip, c = (column + WIDTH) // WIDTH, (column + WIDTH) % WIDTH
            return [cols[strip, h, unit, c, half] for half in range(2)]

        def put(column, new):
            for half in range(2):
                done[h, column, v, half] = new[half]
                row = ((v * 16 + h * 8) * 2 + half) * 8 + column
                nat[pl.ds(row, 8, stride=16), :] = new[half]

        diffuse(
            lambda column: load(VAR + v, column),
            lambda column: load(SX, column),
            lambda column: load(SY, column),
            put,
            lane,
        )

    for h in range(2):
        for unit in range(4):
            for i in range(2):
                halo_copy(h, i, unit).wait_recv()
            if unit >= VAR:
                run_block(h, unit - VAR)

    def slot(b):
        return win_ref.at[pl.ds(pl.multiple_of(b * 64, 64), 64)]

    def target(i):
        return i // 4 * 4 + lax.rem(lax.rem(band, 4) + lax.rem(i, 4), 4)

    def band_copy(i):
        return pltpu.make_async_remote_copy(
            src_ref=send_buf.at[i],
            dst_ref=slot(band),
            send_sem=as_sem.at[i],
            recv_sem=ar_sem.at[band],
            device_id=(target(i), lon),
            device_id_type=MESH,
        )

    def send(i, carry):
        b = target(i)
        start = st[b]
        for c in range(WIDTH):
            parts = []
            for q in range(4):
                v, h = q // 2, q % 2
                x = jnp.where(lane >= start, done[h, c, v, 0], done[h, c, v, 1])
                parts.append(roll(x, (32 * q + 256 - start) & 127))
            send_buf[i, pl.ds(c * 8, 8), :] = jnp.where(
                lane < 64,
                jnp.where(lane < 32, parts[0], parts[1]),
                jnp.where(lane < 96, parts[2], parts[3]),
            )

        @pl.when(b != band)
        def _():
            band_copy(i).start()

        @pl.when(b == band)
        def _():
            pltpu.make_async_copy(send_buf.at[i], slot(band), ar_sem.at[band]).start()

        return carry

    lax.fori_loop(0, n_band, send, 0)

    for v in range(2):
        for level in range(16):
            at = (v * 16 + level) * 16
            value = nat[at:at + 16, :]
            for o in range(5):
                if 0 <= level + o - 2 < 16:
                    beside = at + (o - 2) * 16
                    value = value + filt[o, v, level] * nat[beside:beside + 16, :]
            inc_ref[at:at + 16, :] = value

    for h in range(2):
        for unit in range(4):
            for i in range(2):
                halo_copy(h, i, unit).wait_send()

    def sent(i, carry):
        @pl.when(target(i) != band)
        def _():
            band_copy(i).wait_send()

        return carry

    def arrive(b, carry):
        pltpu.make_async_copy(send_buf.at[0], slot(b), ar_sem.at[b]).wait()
        return carry

    lax.fori_loop(0, n_band, sent, 0)
    lax.fori_loop(0, n_band, arrive, 0)


def filter_kernel(
    rows_ref, filt_ref, win_ref, inc_ref, out_inc_ref, bf_ref,
    rows, filt, band_nat, out_bf, in_sem, out_sem,
):
    outs = [pltpu.make_async_copy(inc_ref, out_inc_ref, out_sem.at[2])]
    scalars = [
        pltpu.make_async_copy(rows_ref, rows, in_sem.at[0]),
        pltpu.make_async_copy(filt_ref, filt, in_sem.at[1]),
    ]
    for copy in scalars + outs:
        copy.start()
    for s in range(8):
        flat = win_ref[pl.ds(s, LANES, stride=8), :].T
        for q in range(4):
            v, h = q // 2, q % 2
            band_nat[v, h * 8 + s] = flat[q * CAP:(q + 1) * CAP, :]
    for copy in scalars:
        copy.wait()

    inside = lax.broadcasted_iota(jnp.int32, (CAP, LANES), 0) < rows[lax.axis_index("band")]
    for v in range(2):
        for level in range(16):
            value = band_nat[v, level]
            for o in range(5):
                if 0 <= level + o - 2 < 16:
                    value = value + filt[o, v, level] * band_nat[v, level + o - 2]
            at = (v * 16 + level) * CAP
            out_bf[at:at + CAP, :] = jnp.where(inside, value, 0.0)
        outs.append(
            pltpu.make_async_copy(
                out_bf.at[pl.ds(v * 512, 512)], bf_ref.at[pl.ds(v * 512, 512)], out_sem.at[v]
            )
        )
        outs[-1].start()
    for copy in outs:
        copy.wait()


def tiles(a):
    n = a.size // 2048
    return jnp.transpose(a.reshape(n, 8, 2, LANES), (0, 2, 1, 3)).reshape(n * 16, LANES)


def shards(background, scale_x, scale_y, filter_bands, band_rows):
    f32 = jnp.float32
    any_space = pl.BlockSpec(memory_space=pl.ANY)
    hbm = pl.BlockSpec(memory_space=pltpu.HBM)
    resident = pl.BlockSpec(memory_space=pltpu.VMEM)
    vmem = pltpu.VMEM
    dma = pltpu.SemaphoreType.DMA

    def stay(a):
        return pltpu.with_memory_space_constraint(a, pltpu.HBM)

    filters = jnp.transpose(filter_bands, (1, 0, 2))
    win, inc = pl.pallas_call(
        strips_kernel,
        out_shape=(
            jax.ShapeDtypeStruct((1024, LANES), f32),
            jax.ShapeDtypeStruct((512, LANES), f32),
        ),
        in_specs=[hbm] * 5,
        out_specs=(resident, resident),
        scratch_shapes=[
            vmem((4, 2, 128, LANES), f32),
            vmem((3, 2, 4, WIDTH, 2, 8, LANES), f32),
            vmem((2, WIDTH, 2, 2, 8, LANES), f32),
            vmem((512, LANES), f32),
            vmem((16, 64, LANES), f32),
            pltpu.SMEM((16,), jnp.int32),
            pltpu.SMEM((5, 2, 16), f32),
            pltpu.SMEM((16,), jnp.int32),
            pltpu.SemaphoreType.REGULAR((3,)),
            dma((5,)),
            dma((2, 2, 4)),
            dma((2, 2, 4)),
            dma((16,)),
            dma((16,)),
        ],
        compiler_params=pltpu.CompilerParams(
            collective_id=0, has_side_effects=True, vmem_limit_bytes=16 << 20
        ),
    )(
        stay(band_rows),
        stay(filters),
        stay(tiles(background).reshape(2, 2, 128, LANES)),
        stay(tiles(scale_x).reshape(2, 128, LANES)),
        stay(tiles(scale_y).reshape(2, 128, LANES)),
    )
    inc, bf = pl.pallas_call(
        filter_kernel,
        out_shape=(
            jax.ShapeDtypeStruct((512, LANES), f32),
            jax.ShapeDtypeStruct((1024, LANES), f32),
        ),
        in_specs=[any_space, any_space, resident, resident],
        out_specs=(hbm, hbm),
        scratch_shapes=[
            pltpu.SMEM((16,), jnp.int32),
            pltpu.SMEM((5, 2, 16), f32),
            vmem((2, 16, CAP, LANES), f32),
            vmem((1024, LANES), f32),
            dma((2,)),
            dma((3,)),
        ],
        compiler_params=pltpu.CompilerParams(vmem_limit_bytes=16 << 20),
    )(band_rows, filters, win, inc)
    inc = jnp.transpose(inc.reshape(32, 2, 8, LANES), (0, 2, 1, 3))
    return inc.reshape(background.shape), bf.reshape(2, 16, CAP, LANES)


def solution(mesh):
    strips = P(None, None, ("lon", "band"), None)
    faces = P(None, ("lon", "band"), None)
    return jax.shard_map(
        shards,
        mesh=mesh,
        in_specs=(strips, faces, faces, P(), P()),
        out_specs=(strips, P(None, None, "band", "lon")),
        check_vma=False,
    )
```

```python
import jax
import jax.numpy as jnp
from jax import lax
from jax.experimental import pallas as pl
from jax.experimental.pallas import tpu as pltpu
from jax.sharding import PartitionSpec as P

MESH = pl.DeviceIdType.MESH
STEPS = 8
CAP = 32
WIDTH = 8
LANES = 128
LEFT, OWN, RIGHT = 0, 1, 2
SX, SY, VAR = 0, 1, 2


def roll(x, shift):
    return pltpu.roll(x, shift, x.ndim - 1)


def diffuse(get_field, get_sx, get_sy, put, lane):
    last, first = lane == LANES - 1, lane == 0
    held = [None] * STEPS
    flux = [None] * STEPS

    def push(step, column, field):
        if step == STEPS:
            put(column, field)
            return
        before, west = held[step], flux[step]
        held[step] = field
        if before is None:
            return
        p = column - 1
        sx = get_sx(p)
        east = [sx[i] * (field[i] - before[i]) for i in range(2)]
        flux[step] = east
        if west is None:
            return
        sy = get_sy(p)
        ra, rb = roll(before[0], LANES - 1), roll(before[1], LANES - 1)
        up = [jnp.where(last, rb, ra), rb]
        north = [sy[i] * (up[i] - before[i]) for i in range(2)]
        qa, qb = roll(north[0], 1), roll(north[1], 1)
        south = [jnp.where(first, qb, qa), jnp.where(first, qa, qb)]
        new = [before[i] + east[i] - west[i] + north[i] - south[i] for i in range(2)]
        push(step + 1, p, new)

    for column in range(-STEPS, WIDTH + STEPS):
        push(0, column, get_field(column))


def torus(band):
    z, y = band // 4, lax.rem(band, 4)
    return [
        lax.rem(z + 1, 4) * 4 + y,
        lax.rem(z + 3, 4) * 4 + y,
        z * 4 + lax.rem(y + 1, 4),
        z * 4 + lax.rem(y + 3, 4),
    ]


def strips_kernel(
    rows_ref, filt_ref, bg_ref, sx_ref, sy_ref,
    win_ref, inc_ref,
    raw, cols, done, nat, send_buf, rows, filt, st,
    near_sem, in_sem, hs_sem, hr_sem, as_sem, ar_sem,
):
    n_band, n_lon = lax.axis_size("band"), lax.axis_size("lon")
    band, lon = lax.axis_index("band"), lax.axis_index("lon")
    at_end, at_start = band == n_band - 1, band == 0
    right = (
        jnp.where(at_end, 0, band + 1),
        jnp.where(at_end, lax.rem(lon + 1, n_lon), lon),
    )
    left = (
        jnp.where(at_start, n_band - 1, band - 1),
        jnp.where(at_start, lax.rem(lon + n_lon - 1, n_lon), lon),
    )
    near = [(b, lon) for b in torus(band)]

    barrier = pltpu.get_barrier_semaphore()
    for side in [left, right] + near:
        pl.semaphore_signal(barrier, inc=1, device_id=side, device_id_type=MESH)

    copies = [
        pltpu.make_async_copy(sx_ref, raw.at[SX], in_sem.at[0]),
        pltpu.make_async_copy(sy_ref, raw.at[SY], in_sem.at[1]),
        pltpu.make_async_copy(bg_ref, raw.at[pl.ds(VAR, 2)], in_sem.at[2]),
    ]
    scalars = [
        pltpu.make_async_copy(rows_ref, rows, in_sem.at[3]),
        pltpu.make_async_copy(filt_ref, filt, in_sem.at[4]),
    ]
    for copy in copies + scalars:
        copy.start()

    def halo_copy(h, i, unit):
        device, strip = ((left, RIGHT), (right, LEFT))[i]
        first, count = 0, WIDTH
        if i == 0 and unit in (SX, SY):
            count = WIDTH - 1
        elif i == 1 and unit == SY:
            first, count = 1, WIDTH - 1
        return pltpu.make_async_remote_copy(
            src_ref=cols.at[OWN, h, unit, pl.ds(first, count)],
            dst_ref=cols.at[strip, h, unit, pl.ds(first, count)],
            send_sem=hs_sem.at[h, i, unit],
            recv_sem=hr_sem.at[h, i, unit],
            device_id=device,
            device_id_type=MESH,
        )

    lane = lax.broadcasted_iota(jnp.int32, (8, LANES), 1)
    for h in range(2):
        for unit in range(4):
            if h == 0 and unit < 3:
                copies[unit].wait()
            for c in range(WIDTH):
                for half in range(2):
                    tile = raw[unit, h, pl.ds(half * 8 + c, 8, stride=16), :]
                    if unit == SY and half == 1:
                        tile = jnp.where(lane == LANES - 1, 0.0, tile)
                    cols[OWN, h, unit, c, half] = tile
        if h == 0:
            pl.semaphore_wait(barrier, 6)
        for unit in range(4):
            for i in range(2):
                halo_copy(h, i, unit).start()

    for hop in range(3):
        for peer in near:
            pl.semaphore_signal(
                near_sem.at[hop], inc=1, device_id=peer, device_id_type=MESH
            )
        pl.semaphore_wait(near_sem.at[hop], 4)

    for copy in scalars:
        copy.wait()
    total = jnp.int32(0)
    for b in range(16):
        st[b] = total
        total = total + rows[b]

    def run_block(h, v):
        def load(unit, column):
            strip, c = (column + WIDTH) // WIDTH, (column + WIDTH) % WIDTH
            return [cols[strip, h, unit, c, half] for half in range(2)]

        def put(column, new):
            for half in range(2):
                turn = 32 * (2 * v + h)
                done[column, 2 * v + h, half] = roll(new[half], turn) if turn else new[half]
                row = ((v * 16 + h * 8) * 2 + half) * 8 + column
                nat[pl.ds(row, 8, stride=16), :] = new[half]

        def get_field(column):
            if column == -WIDTH:
                for i in range(2):
                    for unit in ((SX, SY, VAR), (VAR + 1,))[v]:
                        halo_copy(h, i, unit).wait_recv()
            return load(VAR + v, column)

        diffuse(
            get_field,
            lambda column: load(SX, column),
            lambda column: load(SY, column),
            put,
            lane,
        )

    for h in range(2):
        for v in range(2):
            run_block(h, v)

    def slot(b):
        return win_ref.at[pl.ds(pl.multiple_of(b * 64, 64), 64)]

    def target(i):
        return i // 4 * 4 + lax.rem(lax.rem(band, 4) + lax.rem(i, 4), 4)

    def band_copy(i):
        return pltpu.make_async_remote_copy(
            src_ref=send_buf.at[i],
            dst_ref=slot(band),
            send_sem=as_sem.at[i],
            recv_sem=ar_sem.at[band],
            device_id=(target(i), lon),
            device_id_type=MESH,
        )

    def send(i, carry):
        b = target(i)
        start = st[b]
        place = (lane + (256 - start)) & 127
        top, second, fourth = place < 64, place < 32, place < 96
        low = ((lane + 128 - 32 * (place // 32)) & 127) >= start
        for c in range(WIDTH):
            both = []
            for half in range(2):
                x = [done[c, q, half] for q in range(4)]
                both.append(
                    jnp.where(top, jnp.where(second, x[0], x[1]), jnp.where(fourth, x[2], x[3]))
                )
            x = jnp.where(low, both[0], both[1])
            send_buf[i, pl.ds(c * 8, 8), :] = roll(x, (256 - start) & 127)

        @pl.when(b != band)
        def _():
            band_copy(i).start()

        @pl.when(b == band)
        def _():
            pltpu.make_async_copy(send_buf.at[i], slot(band), ar_sem.at[band]).start()

        return carry

    lax.fori_loop(0, n_band, send, 0)

    for v in range(2):
        for level in range(16):
            at = (v * 16 + level) * 16
            value = nat[at:at + 16, :]
            for o in range(5):
                if 0 <= level + o - 2 < 16:
                    beside = at + (o - 2) * 16
                    value = value + filt[o, v, level] * nat[beside:beside + 16, :]
            inc_ref[at:at + 16, :] = value

    for h in range(2):
        for unit in range(4):
            for i in range(2):
                halo_copy(h, i, unit).wait_send()

    def sent(i, carry):
        @pl.when(target(i) != band)
        def _():
            band_copy(i).wait_send()

        return carry

    def arrive(b, carry):
        pltpu.make_async_copy(send_buf.at[0], slot(b), ar_sem.at[b]).wait()
        return carry

    lax.fori_loop(0, n_band, sent, 0)
    lax.fori_loop(0, n_band, arrive, 0)


def filter_kernel(
    rows_ref, filt_ref, win_ref, inc_ref, out_inc_ref, bf_ref,
    rows, filt, band_nat, out_bf, in_sem, out_sem,
):
    outs = [pltpu.make_async_copy(inc_ref, out_inc_ref, out_sem.at[2])]
    scalars = [
        pltpu.make_async_copy(rows_ref, rows, in_sem.at[0]),
        pltpu.make_async_copy(filt_ref, filt, in_sem.at[1]),
    ]
    for copy in scalars + outs:
        copy.start()
    for s in range(8):
        flat = win_ref[pl.ds(s, LANES, stride=8), :].T
        for q in range(4):
            v, h = q // 2, q % 2
            band_nat[v, h * 8 + s] = flat[q * CAP:(q + 1) * CAP, :]
    for copy in scalars:
        copy.wait()

    inside = lax.broadcasted_iota(jnp.int32, (CAP, LANES), 0) < rows[lax.axis_index("band")]
    for v in range(2):
        for level in range(16):
            value = band_nat[v, level]
            for o in range(5):
                if 0 <= level + o - 2 < 16:
                    value = value + filt[o, v, level] * band_nat[v, level + o - 2]
            at = (v * 16 + level) * CAP
            out_bf[at:at + CAP, :] = jnp.where(inside, value, 0.0)
        outs.append(
            pltpu.make_async_copy(
                out_bf.at[pl.ds(v * 512, 512)], bf_ref.at[pl.ds(v * 512, 512)], out_sem.at[v]
            )
        )
        outs[-1].start()
    for copy in outs:
        copy.wait()


def tiles(a):
    n = a.size // 2048
    return jnp.transpose(a.reshape(n, 8, 2, LANES), (0, 2, 1, 3)).reshape(n * 16, LANES)


def shards(background, scale_x, scale_y, filter_bands, band_rows):
    f32 = jnp.float32
    hbm = pl.BlockSpec(memory_space=pltpu.HBM)
    resident = pl.BlockSpec(memory_space=pltpu.VMEM)
    vmem = pltpu.VMEM
    dma = pltpu.SemaphoreType.DMA

    def stay(a):
        return pltpu.with_memory_space_constraint(a, pltpu.HBM)

    filters = jnp.transpose(filter_bands, (1, 0, 2))
    win, inc = pl.pallas_call(
        strips_kernel,
        out_shape=(
            jax.ShapeDtypeStruct((1024, LANES), f32),
            jax.ShapeDtypeStruct((512, LANES), f32),
        ),
        in_specs=[hbm] * 5,
        out_specs=(resident, resident),
        scratch_shapes=[
            vmem((4, 2, 128, LANES), f32),
            vmem((3, 2, 4, WIDTH, 2, 8, LANES), f32),
            vmem((WIDTH, 4, 2, 8, LANES), f32),
            vmem((512, LANES), f32),
            vmem((16, 64, LANES), f32),
            pltpu.SMEM((16,), jnp.int32),
            pltpu.SMEM((5, 2, 16), f32),
            pltpu.SMEM((16,), jnp.int32),
            pltpu.SemaphoreType.REGULAR((3,)),
            dma((5,)),
            dma((2, 2, 4)),
            dma((2, 2, 4)),
            dma((16,)),
            dma((16,)),
        ],
        compiler_params=pltpu.CompilerParams(
            collective_id=0, has_side_effects=True, vmem_limit_bytes=16 << 20
        ),
    )(
        stay(band_rows),
        stay(filters),
        stay(tiles(background).reshape(2, 2, 128, LANES)),
        stay(tiles(scale_x).reshape(2, 128, LANES)),
        stay(tiles(scale_y).reshape(2, 128, LANES)),
    )
    inc, bf = pl.pallas_call(
        filter_kernel,
        out_shape=(
            jax.ShapeDtypeStruct((512, LANES), f32),
            jax.ShapeDtypeStruct((1024, LANES), f32),
        ),
        in_specs=[hbm, hbm, resident, resident],
        out_specs=(hbm, hbm),
        scratch_shapes=[
            pltpu.SMEM((16,), jnp.int32),
            pltpu.SMEM((5, 2, 16), f32),
            vmem((2, 16, CAP, LANES), f32),
            vmem((1024, LANES), f32),
            dma((2,)),
            dma((3,)),
        ],
        compiler_params=pltpu.CompilerParams(vmem_limit_bytes=16 << 20),
    )(stay(band_rows), stay(filters), win, inc)
    inc = jnp.transpose(inc.reshape(32, 2, 8, LANES), (0, 2, 1, 3))
    return inc.reshape(background.shape), bf.reshape(2, 16, CAP, LANES)


def solution(mesh):
    strips = P(None, None, ("lon", "band"), None)
    faces = P(None, ("lon", "band"), None)
    return jax.shard_map(
        shards,
        mesh=mesh,
        in_specs=(strips, faces, faces, P(), P()),
        out_specs=(strips, P(None, None, "band", "lon")),
        check_vma=False,
    )
```

```python
import jax
import jax.numpy as jnp
from jax import lax
from jax.experimental import pallas as pl
from jax.experimental.pallas import tpu as pltpu
from jax.sharding import PartitionSpec as P

MESH = pl.DeviceIdType.MESH
STEPS = 8
CAP = 32
WIDTH = 8
LANES = 128
LEFT, OWN, RIGHT = 0, 1, 2
SX, SY, VAR = 0, 1, 2


def roll(x, shift):
    return pltpu.roll(x, shift, x.ndim - 1)


def diffuse(get_field, get_sx, get_sy, get_behind, put, lane):
    last, first = lane == LANES - 1, lane == 0
    held = [None] * STEPS
    flux = [None] * STEPS

    def push(step, column, field):
        if step == STEPS:
            put(column, field)
            return
        before, west = held[step], flux[step]
        held[step] = field
        if before is None:
            return
        p = column - 1
        sx = get_sx(p)
        east = [sx[i] * (field[i] - before[i]) for i in range(2)]
        flux[step] = east
        if west is None:
            return
        sy, behind = get_sy(p), get_behind(p)
        ra, rb = roll(before[0], LANES - 1), roll(before[1], LANES - 1)
        up = [jnp.where(last, rb, ra), rb]
        qa, qb = roll(before[0], 1), roll(before[1], 1)
        down = [qa, jnp.where(first, qa, qb)]
        north = [sy[i] * (up[i] - before[i]) for i in range(2)]
        south = [behind[i] * (before[i] - down[i]) for i in range(2)]
        new = [before[i] + east[i] - west[i] + north[i] - south[i] for i in range(2)]
        push(step + 1, p, new)

    for column in range(-STEPS, WIDTH + STEPS):
        push(0, column, get_field(column))


def torus(band):
    z, y = band // 4, lax.rem(band, 4)
    return [
        lax.rem(z + 1, 4) * 4 + y,
        lax.rem(z + 3, 4) * 4 + y,
        z * 4 + lax.rem(y + 1, 4),
        z * 4 + lax.rem(y + 3, 4),
    ]


def strips_kernel(
    rows_ref, filt_ref, bg_ref, sx_ref, sy_ref,
    win_ref, inc_ref,
    raw, cols, row_behind, done, nat, send_buf, rows, filt, st,
    near_sem, in_sem, hs_sem, hr_sem, as_sem, ar_sem,
):
    n_band, n_lon = lax.axis_size("band"), lax.axis_size("lon")
    band, lon = lax.axis_index("band"), lax.axis_index("lon")
    at_end, at_start = band == n_band - 1, band == 0
    right = (
        jnp.where(at_end, 0, band + 1),
        jnp.where(at_end, lax.rem(lon + 1, n_lon), lon),
    )
    left = (
        jnp.where(at_start, n_band - 1, band - 1),
        jnp.where(at_start, lax.rem(lon + n_lon - 1, n_lon), lon),
    )
    near = [(b, lon) for b in torus(band)]

    barrier = pltpu.get_barrier_semaphore()
    for side in [left, right] + near:
        pl.semaphore_signal(barrier, inc=1, device_id=side, device_id_type=MESH)

    copies = [
        pltpu.make_async_copy(sx_ref, raw.at[SX], in_sem.at[0]),
        pltpu.make_async_copy(sy_ref, raw.at[SY], in_sem.at[1]),
        pltpu.make_async_copy(bg_ref, raw.at[pl.ds(VAR, 2)], in_sem.at[2]),
    ]
    scalars = [
        pltpu.make_async_copy(rows_ref, rows, in_sem.at[3]),
        pltpu.make_async_copy(filt_ref, filt, in_sem.at[4]),
    ]
    for copy in copies + scalars:
        copy.start()

    def halo_copy(h, i, unit):
        device, strip = ((left, RIGHT), (right, LEFT))[i]
        first, count = 0, WIDTH
        if i == 0 and unit in (SX, SY):
            count = WIDTH - 1
        elif i == 1 and unit == SY:
            first, count = 1, WIDTH - 1
        return pltpu.make_async_remote_copy(
            src_ref=cols.at[OWN, h, unit, pl.ds(first, count)],
            dst_ref=cols.at[strip, h, unit, pl.ds(first, count)],
            send_sem=hs_sem.at[h, i, unit],
            recv_sem=hr_sem.at[h, i, unit],
            device_id=device,
            device_id_type=MESH,
        )

    lane = lax.broadcasted_iota(jnp.int32, (8, LANES), 1)
    for h in range(2):
        for unit in range(4):
            if h == 0 and unit < 3:
                copies[unit].wait()
            for c in range(WIDTH):
                for half in range(2):
                    tile = raw[unit, h, pl.ds(half * 8 + c, 8, stride=16), :]
                    if unit == SY and half == 1:
                        tile = jnp.where(lane == LANES - 1, 0.0, tile)
                    cols[OWN, h, unit, c, half] = tile
        if h == 0:
            pl.semaphore_wait(barrier, 6)
        for unit in range(4):
            for i in range(2):
                halo_copy(h, i, unit).start()

    for hop in range(3):
        for peer in near:
            pl.semaphore_signal(
                near_sem.at[hop], inc=1, device_id=peer, device_id_type=MESH
            )
        pl.semaphore_wait(near_sem.at[hop], 4)

    for copy in scalars:
        copy.wait()
    total = jnp.int32(0)
    for b in range(16):
        st[b] = total
        total = total + rows[b]

    def run_block(h, v):
        def load(unit, column):
            strip, c = (column + WIDTH) // WIDTH, (column + WIDTH) % WIDTH
            return [cols[strip, h, unit, c, half] for half in range(2)]

        def put(column, new):
            for half in range(2):
                turn = 32 * (2 * v + h)
                done[column, 2 * v + h, half] = roll(new[half], turn) if turn else new[half]
                row = ((v * 16 + h * 8) * 2 + half) * 8 + column
                nat[pl.ds(row, 8, stride=16), :] = new[half]

        if v == 0:
            for i in range(2):
                halo_copy(h, i, SX).wait_recv()
                halo_copy(h, i, SY).wait_recv()
            for column in range(1 - WIDTH, 2 * WIDTH - 1):
                low, high = load(SY, column)
                low, high = roll(low, 1), roll(high, 1)
                row_behind[h, column + WIDTH, 0] = jnp.where(lane == 0, high, low)
                row_behind[h, column + WIDTH, 1] = jnp.where(lane == 0, low, high)
        for i in range(2):
            halo_copy(h, i, VAR + v).wait_recv()

        diffuse(
            lambda column: load(VAR + v, column),
            lambda column: load(SX, column),
            lambda column: load(SY, column),
            lambda column: [row_behind[h, column + WIDTH, half] for half in range(2)],
            put,
            lane,
        )

    for h in range(2):
        for v in range(2):
            run_block(h, v)

    def slot(b):
        return win_ref.at[pl.ds(pl.multiple_of(b * 64, 64), 64)]

    def target(i):
        return i

    def band_copy(i):
        return pltpu.make_async_remote_copy(
            src_ref=send_buf.at[i],
            dst_ref=slot(band),
            send_sem=as_sem.at[i],
            recv_sem=ar_sem.at[band],
            device_id=(target(i), lon),
            device_id_type=MESH,
        )

    def send(i, carry):
        b = target(i)
        start = st[b]
        place = (lane + (256 - start)) & 127
        top, second, fourth = place < 64, place < 32, place < 96
        low = ((lane + 128 - 32 * (place // 32)) & 127) >= start
        for c in range(WIDTH):
            both = []
            for half in range(2):
                x = [done[c, q, half] for q in range(4)]
                both.append(
                    jnp.where(top, jnp.where(second, x[0], x[1]), jnp.where(fourth, x[2], x[3]))
                )
            x = jnp.where(low, both[0], both[1])
            send_buf[i, pl.ds(c * 8, 8), :] = roll(x, (256 - start) & 127)

        @pl.when(b != band)
        def _():
            band_copy(i).start()

        @pl.when(b == band)
        def _():
            pltpu.make_async_copy(send_buf.at[i], slot(band), ar_sem.at[band]).start()

        return carry

    lax.fori_loop(0, n_band, send, 0)

    for v in range(2):
        for level in range(16):
            at = (v * 16 + level) * 16
            value = nat[at:at + 16, :]
            for o in range(5):
                if 0 <= level + o - 2 < 16:
                    beside = at + (o - 2) * 16
                    value = value + filt[o, v, level] * nat[beside:beside + 16, :]
            inc_ref[at:at + 16, :] = value

    for h in range(2):
        for unit in range(4):
            for i in range(2):
                halo_copy(h, i, unit).wait_send()

    def sent(i, carry):
        @pl.when(target(i) != band)
        def _():
            band_copy(i).wait_send()

        return carry

    def arrive(b, carry):
        pltpu.make_async_copy(send_buf.at[0], slot(b), ar_sem.at[b]).wait()
        return carry

    lax.fori_loop(0, n_band, sent, 0)
    lax.fori_loop(0, n_band, arrive, 0)


def filter_kernel(
    rows_ref, filt_ref, win_ref, inc_ref, out_inc_ref, bf_ref,
    rows, filt, band_nat, out_bf, in_sem, out_sem,
):
    outs = [pltpu.make_async_copy(inc_ref, out_inc_ref, out_sem.at[2])]
    scalars = [
        pltpu.make_async_copy(rows_ref, rows, in_sem.at[0]),
        pltpu.make_async_copy(filt_ref, filt, in_sem.at[1]),
    ]
    for copy in scalars + outs:
        copy.start()
    for s in range(8):
        flat = win_ref[pl.ds(s, LANES, stride=8), :].T
        for q in range(4):
            v, h = q // 2, q % 2
            band_nat[v, h * 8 + s] = flat[q * CAP:(q + 1) * CAP, :]
    for copy in scalars:
        copy.wait()

    inside = lax.broadcasted_iota(jnp.int32, (CAP, LANES), 0) < rows[lax.axis_index("band")]
    for v in range(2):
        for level in range(16):
            value = band_nat[v, level]
            for o in range(5):
                if 0 <= level + o - 2 < 16:
                    value = value + filt[o, v, level] * band_nat[v, level + o - 2]
            at = (v * 16 + level) * CAP
            out_bf[at:at + CAP, :] = jnp.where(inside, value, 0.0)
        outs.append(
            pltpu.make_async_copy(
                out_bf.at[pl.ds(v * 512, 512)], bf_ref.at[pl.ds(v * 512, 512)], out_sem.at[v]
            )
        )
        outs[-1].start()
    for copy in outs:
        copy.wait()


def tiles(a):
    n = a.size // 2048
    return jnp.transpose(a.reshape(n, 8, 2, LANES), (0, 2, 1, 3)).reshape(n * 16, LANES)


def shards(background, scale_x, scale_y, filter_bands, band_rows):
    f32 = jnp.float32
    hbm = pl.BlockSpec(memory_space=pltpu.HBM)
    resident = pl.BlockSpec(memory_space=pltpu.VMEM)
    vmem = pltpu.VMEM
    dma = pltpu.SemaphoreType.DMA

    def stay(a):
        return pltpu.with_memory_space_constraint(a, pltpu.HBM)

    filters = jnp.transpose(filter_bands, (1, 0, 2))
    win, inc = pl.pallas_call(
        strips_kernel,
        out_shape=(
            jax.ShapeDtypeStruct((1024, LANES), f32),
            jax.ShapeDtypeStruct((512, LANES), f32),
        ),
        in_specs=[hbm] * 5,
        out_specs=(resident, resident),
        scratch_shapes=[
            vmem((4, 2, 128, LANES), f32),
            vmem((3, 2, 4, WIDTH, 2, 8, LANES), f32),
            vmem((2, 3 * WIDTH, 2, 8, LANES), f32),
            vmem((WIDTH, 4, 2, 8, LANES), f32),
            vmem((512, LANES), f32),
            vmem((16, 64, LANES), f32),
            pltpu.SMEM((16,), jnp.int32),
            pltpu.SMEM((5, 2, 16), f32),
            pltpu.SMEM((16,), jnp.int32),
            pltpu.SemaphoreType.REGULAR((3,)),
            dma((5,)),
            dma((2, 2, 4)),
            dma((2, 2, 4)),
            dma((16,)),
            dma((16,)),
        ],
        compiler_params=pltpu.CompilerParams(
            collective_id=0, has_side_effects=True, vmem_limit_bytes=16 << 20
        ),
    )(
        stay(band_rows),
        stay(filters),
        stay(tiles(background).reshape(2, 2, 128, LANES)),
        stay(tiles(scale_x).reshape(2, 128, LANES)),
        stay(tiles(scale_y).reshape(2, 128, LANES)),
    )
    inc, bf = pl.pallas_call(
        filter_kernel,
        out_shape=(
            jax.ShapeDtypeStruct((512, LANES), f32),
            jax.ShapeDtypeStruct((1024, LANES), f32),
        ),
        in_specs=[hbm, hbm, resident, resident],
        out_specs=(hbm, hbm),
        scratch_shapes=[
            pltpu.SMEM((16,), jnp.int32),
            pltpu.SMEM((5, 2, 16), f32),
            vmem((2, 16, CAP, LANES), f32),
            vmem((1024, LANES), f32),
            dma((2,)),
            dma((3,)),
        ],
        compiler_params=pltpu.CompilerParams(vmem_limit_bytes=16 << 20),
    )(stay(band_rows), stay(filters), win, inc)
    inc = jnp.transpose(inc.reshape(32, 2, 8, LANES), (0, 2, 1, 3))
    return inc.reshape(background.shape), bf.reshape(2, 16, CAP, LANES)


def solution(mesh):
    strips = P(None, None, ("lon", "band"), None)
    faces = P(None, ("lon", "band"), None)
    return jax.shard_map(
        shards,
        mesh=mesh,
        in_specs=(strips, faces, faces, P(), P()),
        out_specs=(strips, P(None, None, "band", "lon")),
        check_vma=False,
    )
```

```python
import jax
import jax.numpy as jnp
from jax import lax
from jax.experimental import pallas as pl
from jax.experimental.pallas import tpu as pltpu
from jax.sharding import PartitionSpec as P

MESH = pl.DeviceIdType.MESH
STEPS = 8
CAP = 32
WIDTH = 8
LANES = 128
LEFT, OWN, RIGHT = 0, 1, 2
SX, SY, VAR = 0, 1, 2


def roll(x, shift):
    return pltpu.roll(x, shift, x.ndim - 1)


def diffuse(get_field, get_sx, get_sy, get_behind, put, lane):
    last, first = lane == LANES - 1, lane == 0
    held = [None] * STEPS
    flux = [None] * STEPS

    def push(step, column, field):
        if step == STEPS:
            put(column, field)
            return
        before, west = held[step], flux[step]
        held[step] = field
        if before is None:
            return
        p = column - 1
        sx = get_sx(p)
        east = [sx[i] * (field[i] - before[i]) for i in range(2)]
        flux[step] = east
        if west is None:
            return
        sy, behind = get_sy(p), get_behind(p)
        ra, rb = roll(before[0], LANES - 1), roll(before[1], LANES - 1)
        up = [jnp.where(last, rb, ra), rb]
        qa, qb = roll(before[0], 1), roll(before[1], 1)
        down = [qa, jnp.where(first, qa, qb)]
        north = [sy[i] * (up[i] - before[i]) for i in range(2)]
        south = [behind[i] * (before[i] - down[i]) for i in range(2)]
        new = [before[i] + east[i] - west[i] + north[i] - south[i] for i in range(2)]
        push(step + 1, p, new)

    for column in range(-STEPS, WIDTH + STEPS):
        push(0, column, get_field(column))


def torus(band):
    z, y = band // 4, lax.rem(band, 4)
    return [
        lax.rem(z + 1, 4) * 4 + y,
        lax.rem(z + 3, 4) * 4 + y,
        z * 4 + lax.rem(y + 1, 4),
        z * 4 + lax.rem(y + 3, 4),
    ]


def strips_kernel(
    rows_ref, filt_ref, bg_ref, sx_ref, sy_ref,
    win_ref, inc_ref,
    raw, cols, row_behind, done, nat, send_buf, rows, filt, st,
    near_sem, in_sem, hs_sem, hr_sem, as_sem, ar_sem,
):
    n_band, n_lon = lax.axis_size("band"), lax.axis_size("lon")
    band, lon = lax.axis_index("band"), lax.axis_index("lon")
    at_end, at_start = band == n_band - 1, band == 0
    right = (
        jnp.where(at_end, 0, band + 1),
        jnp.where(at_end, lax.rem(lon + 1, n_lon), lon),
    )
    left = (
        jnp.where(at_start, n_band - 1, band - 1),
        jnp.where(at_start, lax.rem(lon + n_lon - 1, n_lon), lon),
    )
    near = [(b, lon) for b in torus(band)]

    barrier = pltpu.get_barrier_semaphore()
    for side in [left, right] + near:
        pl.semaphore_signal(barrier, inc=1, device_id=side, device_id_type=MESH)

    copies = [
        pltpu.make_async_copy(sx_ref, raw.at[SX], in_sem.at[0]),
        pltpu.make_async_copy(sy_ref, raw.at[SY], in_sem.at[1]),
        pltpu.make_async_copy(bg_ref, raw.at[pl.ds(VAR, 2)], in_sem.at[2]),
    ]
    scalars = [
        pltpu.make_async_copy(rows_ref, rows, in_sem.at[3]),
        pltpu.make_async_copy(filt_ref, filt, in_sem.at[4]),
    ]
    for copy in copies + scalars:
        copy.start()

    def halo_copy(h, i, unit):
        device, strip = ((left, RIGHT), (right, LEFT))[i]
        first, count = 0, WIDTH
        if i == 0 and unit in (SX, SY):
            count = WIDTH - 1
        elif i == 1 and unit == SY:
            first, count = 1, WIDTH - 1
        return pltpu.make_async_remote_copy(
            src_ref=cols.at[OWN, h, unit, pl.ds(first, count)],
            dst_ref=cols.at[strip, h, unit, pl.ds(first, count)],
            send_sem=hs_sem.at[h, i, unit],
            recv_sem=hr_sem.at[h, i, unit],
            device_id=device,
            device_id_type=MESH,
        )

    lane = lax.broadcasted_iota(jnp.int32, (8, LANES), 1)
    for h in range(2):
        for unit in range(4):
            if h == 0 and unit < 3:
                copies[unit].wait()
            for c in range(WIDTH):
                for half in range(2):
                    tile = raw[unit, h, pl.ds(half * 8 + c, 8, stride=16), :]
                    if unit == SY and half == 1:
                        tile = jnp.where(lane == LANES - 1, 0.0, tile)
                    cols[OWN, h, unit, c, half] = tile
        if h == 0:
            pl.semaphore_wait(barrier, 6)
        for unit in range(4):
            for i in range(2):
                halo_copy(h, i, unit).start()

    for hop in range(3):
        for peer in near:
            pl.semaphore_signal(
                near_sem.at[hop], inc=1, device_id=peer, device_id_type=MESH
            )
        pl.semaphore_wait(near_sem.at[hop], 4)

    for copy in scalars:
        copy.wait()
    total = jnp.int32(0)
    for b in range(16):
        st[b] = total
        total = total + rows[b]

    def run_block(h, v):
        def load(unit, column):
            strip, c = (column + WIDTH) // WIDTH, (column + WIDTH) % WIDTH
            return [cols[strip, h, unit, c, half] for half in range(2)]

        def put(column, new):
            for half in range(2):
                turn = 32 * (2 * v + h)
                done[column, 2 * v + h, half] = roll(new[half], turn) if turn else new[half]
                row = ((v * 16 + h * 8) * 2 + half) * 8 + column
                nat[pl.ds(row, 8, stride=16), :] = new[half]

        if v == 0:
            for i in range(2):
                halo_copy(h, i, SX).wait_recv()
                halo_copy(h, i, SY).wait_recv()
            for column in range(1 - WIDTH, 2 * WIDTH - 1):
                low, high = load(SY, column)
                low, high = roll(low, 1), roll(high, 1)
                row_behind[h, column + WIDTH, 0] = jnp.where(lane == 0, high, low)
                row_behind[h, column + WIDTH, 1] = jnp.where(lane == 0, low, high)
        for i in range(2):
            halo_copy(h, i, VAR + v).wait_recv()

        diffuse(
            lambda column: load(VAR + v, column),
            lambda column: load(SX, column),
            lambda column: load(SY, column),
            lambda column: [row_behind[h, column + WIDTH, half] for half in range(2)],
            put,
            lane,
        )

    for h in range(2):
        for v in range(2):
            run_block(h, v)

    def slot(b):
        return win_ref.at[pl.ds(pl.multiple_of(b * 64, 64), 64)]

    def target(i):
        return i

    def band_copy(i):
        return pltpu.make_async_remote_copy(
            src_ref=send_buf.at[i],
            dst_ref=slot(band),
            send_sem=as_sem.at[i],
            recv_sem=ar_sem.at[band],
            device_id=(target(i), lon),
            device_id_type=MESH,
        )

    def send(i, carry):
        b = target(i)
        start = st[b]
        place = (lane + (256 - start)) & 127
        top, second, fourth = place < 64, place < 32, place < 96
        low = ((lane + 128 - 32 * (place // 32)) & 127) >= start
        for c in range(WIDTH):
            both = []
            for half in range(2):
                x = [done[c, q, half] for q in range(4)]
                both.append(
                    jnp.where(top, jnp.where(second, x[0], x[1]), jnp.where(fourth, x[2], x[3]))
                )
            x = jnp.where(low, both[0], both[1])
            send_buf[i, pl.ds(c * 8, 8), :] = roll(x, (256 - start) & 127)

        @pl.when(b != band)
        def _():
            band_copy(i).start()

        @pl.when(b == band)
        def _():
            pltpu.make_async_copy(send_buf.at[i], slot(band), ar_sem.at[band]).start()

        return carry

    lax.fori_loop(0, n_band, send, 0, unroll=2)

    for v in range(2):
        for level in range(16):
            at = (v * 16 + level) * 16
            value = nat[at:at + 16, :]
            for o in range(5):
                if 0 <= level + o - 2 < 16:
                    beside = at + (o - 2) * 16
                    value = value + filt[o, v, level] * nat[beside:beside + 16, :]
            inc_ref[at:at + 16, :] = value

    for h in range(2):
        for unit in range(4):
            for i in range(2):
                halo_copy(h, i, unit).wait_send()

    def sent(i, carry):
        @pl.when(target(i) != band)
        def _():
            band_copy(i).wait_send()

        return carry

    def arrive(b, carry):
        pltpu.make_async_copy(send_buf.at[0], slot(b), ar_sem.at[b]).wait()
        return carry

    lax.fori_loop(0, n_band, sent, 0)
    lax.fori_loop(0, n_band, arrive, 0)


def filter_kernel(
    rows_ref, filt_ref, win_ref, inc_ref, out_inc_ref, bf_ref,
    rows, filt, band_nat, out_bf, in_sem, out_sem,
):
    outs = [pltpu.make_async_copy(inc_ref, out_inc_ref, out_sem.at[4])]
    scalars = [
        pltpu.make_async_copy(rows_ref, rows, in_sem.at[0]),
        pltpu.make_async_copy(filt_ref, filt, in_sem.at[1]),
    ]
    for copy in scalars + outs:
        copy.start()
    for s in range(8):
        flat = win_ref[pl.ds(s, LANES, stride=8), :].T
        for q in range(4):
            v, h = q // 2, q % 2
            band_nat[v, h * 8 + s] = flat[q * CAP:(q + 1) * CAP, :]
    for copy in scalars:
        copy.wait()

    inside = lax.broadcasted_iota(jnp.int32, (CAP, LANES), 0) < rows[lax.axis_index("band")]
    for v in range(2):
        for level in range(16):
            value = band_nat[v, level]
            for o in range(5):
                if 0 <= level + o - 2 < 16:
                    value = value + filt[o, v, level] * band_nat[v, level + o - 2]
            at = (v * 16 + level) * CAP
            out_bf[at:at + CAP, :] = jnp.where(inside, value, 0.0)
            if level % 8 == 7:
                part = pl.ds(at - 7 * CAP, 8 * CAP)
                outs.append(
                    pltpu.make_async_copy(
                        out_bf.at[part], bf_ref.at[part], out_sem.at[2 * v + level // 8]
                    )
                )
                outs[-1].start()
    for copy in outs:
        copy.wait()


def tiles(a):
    n = a.size // 2048
    return jnp.transpose(a.reshape(n, 8, 2, LANES), (0, 2, 1, 3)).reshape(n * 16, LANES)


def shards(background, scale_x, scale_y, filter_bands, band_rows):
    f32 = jnp.float32
    hbm = pl.BlockSpec(memory_space=pltpu.HBM)
    resident = pl.BlockSpec(memory_space=pltpu.VMEM)
    vmem = pltpu.VMEM
    dma = pltpu.SemaphoreType.DMA

    def stay(a):
        return pltpu.with_memory_space_constraint(a, pltpu.HBM)

    filters = jnp.transpose(filter_bands, (1, 0, 2))
    win, inc = pl.pallas_call(
        strips_kernel,
        out_shape=(
            jax.ShapeDtypeStruct((1024, LANES), f32),
            jax.ShapeDtypeStruct((512, LANES), f32),
        ),
        in_specs=[hbm] * 5,
        out_specs=(resident, resident),
        scratch_shapes=[
            vmem((4, 2, 128, LANES), f32),
            vmem((3, 2, 4, WIDTH, 2, 8, LANES), f32),
            vmem((2, 3 * WIDTH, 2, 8, LANES), f32),
            vmem((WIDTH, 4, 2, 8, LANES), f32),
            vmem((512, LANES), f32),
            vmem((16, 64, LANES), f32),
            pltpu.SMEM((16,), jnp.int32),
            pltpu.SMEM((5, 2, 16), f32),
            pltpu.SMEM((16,), jnp.int32),
            pltpu.SemaphoreType.REGULAR((3,)),
            dma((5,)),
            dma((2, 2, 4)),
            dma((2, 2, 4)),
            dma((16,)),
            dma((16,)),
        ],
        compiler_params=pltpu.CompilerParams(
            collective_id=0, has_side_effects=True, vmem_limit_bytes=16 << 20
        ),
    )(
        stay(band_rows),
        stay(filters),
        stay(tiles(background).reshape(2, 2, 128, LANES)),
        stay(tiles(scale_x).reshape(2, 128, LANES)),
        stay(tiles(scale_y).reshape(2, 128, LANES)),
    )
    inc, bf = pl.pallas_call(
        filter_kernel,
        out_shape=(
            jax.ShapeDtypeStruct((512, LANES), f32),
            jax.ShapeDtypeStruct((1024, LANES), f32),
        ),
        in_specs=[hbm, hbm, resident, resident],
        out_specs=(hbm, hbm),
        scratch_shapes=[
            pltpu.SMEM((16,), jnp.int32),
            pltpu.SMEM((5, 2, 16), f32),
            vmem((2, 16, CAP, LANES), f32),
            vmem((1024, LANES), f32),
            dma((2,)),
            dma((5,)),
        ],
        compiler_params=pltpu.CompilerParams(vmem_limit_bytes=16 << 20),
    )(stay(band_rows), stay(filters), win, inc)
    inc = jnp.transpose(inc.reshape(32, 2, 8, LANES), (0, 2, 1, 3))
    return inc.reshape(background.shape), bf.reshape(2, 16, CAP, LANES)


def solution(mesh):
    strips = P(None, None, ("lon", "band"), None)
    faces = P(None, ("lon", "band"), None)
    return jax.shard_map(
        shards,
        mesh=mesh,
        in_specs=(strips, faces, faces, P(), P()),
        out_specs=(strips, P(None, None, "band", "lon")),
        check_vma=False,
    )
```
